32 devices in a mesh: blk: 16 (over z, y, core), rep: 2 (over x).
Axes of the slice: x: 2, y: 2, z: 4, core: 2. Of those that a mesh axis runs over, the one named last changes fastest.
Arguments:
- features: bfloat16 [32768, 256], P(('blk', 'rep')), may hold values from -6 to 6
- aggregated: bfloat16 [32768, 256], P(('blk', 'rep')), may hold values from -6 to 6
- out_grad: bfloat16 [32768, 256], P(('blk', 'rep')), may hold values from -6 to 6
- w_self: bfloat16 [256, 256], replicated, may hold values from -0.375 to 0.375
- w_neigh: bfloat16 [256, 256], replicated, may hold values from -0.375 to 0.375
- tiles: bfloat16 [16, 16, 8, 128, 128], P('blk'), may hold values from -0.0625 to 0.0625
- tile_rows: int32 [16, 16, 8], P('blk'), may hold values from 0 to 15
- tile_cols: int32 [16, 16, 8], P('blk'), may hold values from 0 to 15
- tile_counts: int32 [16, 16], P('blk'), may hold values from 0 to 8, as said below
Outputs:
- feature_grad: float32 [32768, 256], P(('blk', 'rep'))
- self_grad: float32 [256, 256], replicated
- neigh_grad: float32 [256, 256], replicated
The draws below stay inside these ranges and needn't reach their ends.
Inputs may be any that keep to these rules, and one draw needn't show every extreme that they name: `tile_counts`: at most 8; some pair of blocks uses all 8 slots; tiles, rows and columns of slots beyond the count carry no meaning.
All inputs are finite; a program needn't handle non-finite values.
Results may differ from the reference program's by a relative error of at most 0.00082.
Values may be sent and summed in bfloat16 or wider, within the bound.
A program may use at most 64 MiB of HBM per device.

```python
import jax
import jax.numpy as jnp
from jax import lax

F = 256
TILE = 128
TB = 16
SLOTS = 8
VERTS = 32768
N_BLK = 16


def draw_tile_counts(key, part):
    inner = jax.random.fold_in(key, 11)
    first_key, second_key = jax.random.split(inner)
    base = jax.random.randint(first_key, (N_BLK, N_BLK), SLOTS // 2, SLOTS + 1)
    ceiling = SLOTS - jnp.arange(N_BLK, dtype=jnp.int32) * (SLOTS // 2) // N_BLK
    counts = jnp.minimum(base, ceiling[:, None])
    column = jax.random.randint(second_key, (), 0, N_BLK)
    counts = counts.at[0, column].set(SLOTS)
    return counts.astype(jnp.int32)


def place_ends(result, own_key, low, largest):
    spot = [jax.random.randint(jax.random.fold_in(own_key, axis), (), 0, length) for axis, length in enumerate(result.shape)]
    longest = result.shape.index(max(result.shape))
    next_to = spot[:longest] + [(spot[longest] + 1) % result.shape[longest]] + spot[longest + 1:]
    return result.at[tuple(spot)].set(low).at[tuple(next_to)].set(largest)


def shard_levels(own_key, extent, cuts, low, top_value):
    factor_of, own = 1.0, jax.random.fold_in(own_key, 6)
    for dim, shards_of in cuts:
        draws = jnp.exp(jax.random.uniform(jax.random.fold_in(own, dim), (shards_of,), jnp.float32, low / len(cuts), top_value / len(cuts)))
        factor_of = factor_of * jnp.repeat(draws, extent[dim] // shards_of).reshape([-1 if axis == dim else 1 for axis in range(len(extent))])
    return factor_of


def scatter_about(stream_key, dims, deviation, reach, cuts=(), held_as=jnp.bfloat16):
    drawn = jax.random.normal(stream_key, dims, jnp.float32) * deviation
    if len(cuts) > 0:
        drawn = shard_levels(stream_key, dims, cuts, -0.22, 0.18) * drawn
    return jnp.clip(drawn, min=-reach, max=reach).astype(held_as)


def setup_inputs(seed: int = 0) -> dict:
    arg_keys = jax.random.split(jax.random.key(seed), 10)
    return {
        "features": scatter_about(arg_keys[0], (VERTS, F), 1.0, 6.0, ((0, 32),)),
        "aggregated": scatter_about(arg_keys[1], (VERTS, F), 1.0, 6.0, ((0, 32),)),
        "out_grad": scatter_about(arg_keys[2], (VERTS, F), 1.0, 6.0, ((0, 32),)),
        "w_self": scatter_about(arg_keys[3], (F, F), F ** -0.5, 0.375),
        "w_neigh": scatter_about(arg_keys[4], (F, F), F ** -0.5, 0.375),
        "tiles": scatter_about(arg_keys[5], (N_BLK, N_BLK, SLOTS, TILE, TILE), (TILE * SLOTS * N_BLK // 2) ** -0.5, 0.0625, ((0, 16),)),
        "tile_rows": place_ends(jax.random.randint(arg_keys[6], (N_BLK, N_BLK, SLOTS), 0, TB), jax.random.fold_in(arg_keys[6], 1), 0, TB - 1).astype(jnp.int32),
        "tile_cols": place_ends(jax.random.randint(arg_keys[7], (N_BLK, N_BLK, SLOTS), 0, TB), jax.random.fold_in(arg_keys[7], 1), 0, TB - 1).astype(jnp.int32),
        "tile_counts": draw_tile_counts(jax.random.fold_in(arg_keys[9], 71), 0),
    }


def reference(features, aggregated, out_grad, w_self, w_neigh, tiles, tile_rows, tile_cols, tile_counts):
    message = jnp.dot(out_grad, w_neigh.T, preferred_element_type=jnp.float32).astype(jnp.bfloat16)
    pieces_all = message.reshape(N_BLK * TB, TILE, F)

    def one_block(block_index):
        blocks = tiles[block_index].reshape(N_BLK * SLOTS, TILE, TILE).astype(jnp.float32)
        index = (jnp.arange(N_BLK, dtype=jnp.int32)[:, None] * TB + tile_cols[block_index]).reshape(-1).astype(jnp.int32)
        pieces = pieces_all[index].astype(jnp.float32)
        products = jnp.einsum("kpq,kqf->kpf", blocks, pieces)
        live = (jnp.arange(SLOTS, dtype=jnp.int32)[None, :] < tile_counts[block_index][:, None]).reshape(-1)
        products = jnp.where(live[:, None, None], products, jnp.zeros_like(products))
        start = jnp.zeros((TB, TILE, F), products.dtype)
        return start.at[tile_rows[block_index].reshape(-1)].add(products)

    spread = lax.map(one_block, jnp.arange(N_BLK, dtype=jnp.int32)).reshape(N_BLK * TB * TILE, F)
    feature_grad = jnp.dot(out_grad, w_self.T, preferred_element_type=jnp.float32) + spread
    scale = VERTS ** -0.5
    contract = (((0,), (0,)), ((), ()))
    self_grad = lax.dot_general(features, out_grad, contract, preferred_element_type=jnp.float32) * scale
    neigh_grad = lax.dot_general(aggregated, out_grad, contract, preferred_element_type=jnp.float32) * scale
    return (feature_grad, self_grad, neigh_grad)
```

```python
import functools

import jax
import jax.numpy as jnp
from jax import lax
from jax.experimental import pallas as pl
from jax.experimental.pallas import tpu as pltpu
from jax.sharding import PartitionSpec as P

MESH = pl.DeviceIdType.MESH
CORES, ROWS_Y = 2, 2


def gather_kernel(blocks, own_ref, other_ref, g_ref, send_sem, recv_sem, x_sem, local_sem):
    b = lax.axis_index("blk")
    r = lax.axis_index("rep")
    line = blocks // (CORES * ROWS_Y)
    plane = CORES * ROWS_Y
    z, y, c = b // plane, (b // CORES) % ROWS_Y, b % CORES
    near_x = (b, 1 - r)
    near_core = (z * plane + y * CORES + (1 - c), r)
    near_y = (z * plane + (1 - y) * CORES + c, r)
    up, down = (b + plane, r), (b - plane, r)
    has_up, has_down = z < line - 1, z > 0

    barrier = pltpu.get_barrier_semaphore()
    for device in (near_x, near_core, near_y):
        pl.semaphore_signal(barrier, inc=1, device_id=device, device_id_type=MESH)

    @pl.when(has_up)
    def _():
        pl.semaphore_signal(barrier, inc=1, device_id=up, device_id_type=MESH)

    @pl.when(has_down)
    def _():
        pl.semaphore_signal(barrier, inc=1, device_id=down, device_id_type=MESH)

    expected = 3 + jnp.where(has_up, 1, 0) + jnp.where(has_down, 1, 0)
    pl.semaphore_wait(barrier, expected)

    def send(src, block, share, way, device):
        return pltpu.make_async_remote_copy(
            src_ref=src,
            dst_ref=g_ref.at[block, share],
            send_sem=send_sem.at[way, block, share],
            recv_sem=recv_sem.at[block, share],
            device_id=device,
            device_id_type=MESH,
        )

    def arrived(block, share):
        send(g_ref.at[block, share], block, share, 0, near_core).wait_recv()

    x_copy = pltpu.make_async_remote_copy(
        src_ref=other_ref,
        dst_ref=g_ref.at[b, r],
        send_sem=x_sem,
        recv_sem=recv_sem.at[b, r],
        device_id=near_x,
        device_id_type=MESH,
    )
    x_copy.start()
    keep = pltpu.make_async_copy(own_ref, g_ref.at[b, r], local_sem)
    keep.start()

    def spread_out(src, block, share, go_up, go_down):
        @pl.when(go_up)
        def _():
            send(src, block, share, 0, up).start()

        @pl.when(go_down)
        def _():
            send(src, block, share, 1, down).start()

        send(src, block, share, 2, near_y).start()
        send(src, block, share, 3, near_core).start()

    shares = (r, 1 - r)
    never = z < 0
    spread_out(own_ref, b, r, has_up, has_down)
    arrived(b, 1 - r)
    spread_out(g_ref.at[b, 1 - r], b, 1 - r, has_up, has_down)

    def from_y(distance, share):
        for sign in (-1, 1) if distance else (0,):
            other = z + sign * distance

            @pl.when((other >= 0) & (other < line))
            def _():
                block = other * plane + (1 - y) * CORES + c
                arrived(block, share)
                send(g_ref.at[block, share], block, share, 3, near_core).start()

    for distance in range(1, line):
        for share in shares:

            @pl.when(z - distance >= 0)
            def _():
                block = b - distance * plane
                arrived(block, share)
                spread_out(g_ref.at[block, share], block, share, has_up, never)

            @pl.when(z + distance < line)
            def _():
                block = b + distance * plane
                arrived(block, share)
                spread_out(g_ref.at[block, share], block, share, never, has_down)

        for share in shares:
            from_y(distance - 1, share)
    for share in shares:
        from_y(line - 1, share)

    keep.wait()
    x_copy.wait_send()
    for zz in range(line):
        for share in shares:
            for yy in (y, 1 - y):
                mine = zz * plane + yy * CORES + c
                arrived(zz * plane + yy * CORES + (1 - c), share)
                send(own_ref, mine, share, 3, near_core).wait_send()
            block = zz * plane + y * CORES + c
            send(own_ref, block, share, 2, near_y).wait_send()

            @pl.when((zz <= z) & has_up)
            def _():
                send(own_ref, block, share, 0, up).wait_send()

            @pl.when((zz >= z) & has_down)
            def _():
                send(own_ref, block, share, 1, down).wait_send()


def gather(own, other, blocks, copies):
    rows, width = own.shape
    return pl.pallas_call(
        functools.partial(gather_kernel, blocks),
        out_shape=jax.ShapeDtypeStruct((blocks, copies, rows, width), own.dtype),
        in_specs=[pl.BlockSpec(memory_space=pltpu.VMEM)] * 2,
        out_specs=pl.BlockSpec(memory_space=pl.ANY),
        scratch_shapes=[
            pltpu.SemaphoreType.DMA((4, blocks, copies)),
            pltpu.SemaphoreType.DMA((blocks, copies)),
            pltpu.SemaphoreType.DMA,
            pltpu.SemaphoreType.DMA,
        ],
        compiler_params=pltpu.CompilerParams(collective_id=0, has_side_effects=True),
        cost_estimate=pl.CostEstimate(
            flops=0, bytes_accessed=blocks * copies * rows * width * 20, transcendentals=0
        ),
    )(own, other)


def spread_kernel(rows, cols, counts, tiles_ref, g_ref, o_ref):
    i = pl.program_id(0)
    slots, side = tiles_ref.shape[1], tiles_ref.shape[2]

    @pl.when(i == 0)
    def _():
        o_ref[...] = jnp.zeros_like(o_ref)

    products = []
    for k in range(slots):
        start = pl.multiple_of(cols[i * slots + k] * side, side)
        product = jnp.dot(
            tiles_ref[0, k], g_ref[0, pl.ds(start, side), :], preferred_element_type=jnp.float32
        )
        products.append(jnp.where(k < counts[i], product, jnp.zeros_like(product)))
    for k in range(slots):
        o_ref[rows[i * slots + k]] += products[k]


def spread_of(tiles, gathered, rows, cols, counts):
    blocks, slots, side, _ = tiles.shape
    depth, width = gathered.shape[1:]
    return pl.pallas_call(
        spread_kernel,
        out_shape=jax.ShapeDtypeStruct((depth // side, side, width), jnp.float32),
        grid_spec=pltpu.PrefetchScalarGridSpec(
            num_scalar_prefetch=3,
            grid=(blocks,),
            in_specs=[
                pl.BlockSpec((1, slots, side, side), lambda i, *_: (i, 0, 0, 0)),
                pl.BlockSpec((1, depth, width), lambda i, *_: (i, 0, 0)),
            ],
            out_specs=pl.BlockSpec((depth // side, side, width), lambda i, *_: (0, 0, 0)),
        ),
    )(rows.reshape(-1), cols.reshape(-1), counts.reshape(-1), tiles, gathered)


def by_columns(
    features, aggregated, out_grad, w_self, w_neigh, tiles, tile_rows, tile_cols, tile_counts
):
    blocks, copies = lax.axis_size("blk"), lax.axis_size("rep")
    r = lax.axis_index("rep")
    rows, width = out_grad.shape
    half = width // copies
    side = tiles.shape[-1]
    contract = (((0,), (0,)), ((), ()))
    terms = tuple(
        lax.dot_general(a, out_grad, contract, preferred_element_type=jnp.float32)
        for a in (features, aggregated)
    )
    sums = lax.psum(terms, ("blk", "rep"))
    weights = w_neigh.reshape(copies, half, width)

    def message(which):
        chosen = lax.dynamic_index_in_dim(weights, which, 0, keepdims=False)
        return jnp.dot(out_grad, chosen.T, preferred_element_type=jnp.float32).astype(jnp.bfloat16)

    gathered = gather(message(r), message(1 - r), blocks, copies)
    gathered = gathered.reshape(blocks, copies * rows, half)
    spread = spread_of(tiles[0], gathered, tile_rows[0], tile_cols[0], tile_counts[0])
    spread = spread.reshape(copies, rows, half)
    own = lax.dynamic_index_in_dim(spread, r, 0, keepdims=False)
    sent = lax.dynamic_index_in_dim(spread, 1 - r, 0, keepdims=False).astype(jnp.bfloat16)
    got = lax.ppermute(sent, "rep", [(0, 1), (1, 0)]).astype(jnp.float32)
    left, right = jnp.where(r == 0, own, got), jnp.where(r == 0, got, own)
    self_part = jnp.dot(out_grad, w_self.T, preferred_element_type=jnp.float32)
    scale = (rows * blocks * copies) ** (-0.5)
    feature_grad = self_part + jnp.concatenate([left, right], axis=1)
    return (feature_grad, sums[0] * scale, sums[1] * scale)


def on_device(
    features, aggregated, out_grad, w_self, w_neigh, tiles, tile_rows, tile_cols, tile_counts
):
    block_total = lax.axis_size("blk")
    copies = lax.axis_size("rep")
    replica = lax.axis_index("rep")
    width = out_grad.shape[1]
    side = tiles.shape[-1]
    slots_total = tiles.shape[2]
    share = jnp.dot(out_grad, w_neigh.T, preferred_element_type=jnp.float32).astype(jnp.bfloat16)
    whole = lax.all_gather(share, "rep", axis=0, tiled=True)
    block_rows = whole.shape[0]
    tiles_side = block_rows // side
    pieces_whole = whole.reshape(tiles_side, side, width)
    per_copy = (slots_total + copies - 1) // copies
    slot_ids = replica + copies * jnp.arange(per_copy, dtype=jnp.int32)
    valid = slot_ids < slots_total
    safe = jnp.minimum(slot_ids, slots_total - 1)
    wanted = jnp.take(tile_cols[0], safe, axis=1)
    found = pieces_whole[lax.all_to_all(wanted, "blk", split_axis=0, concat_axis=0, tiled=True)]
    fetched = lax.all_to_all(found, "blk", split_axis=0, concat_axis=0, tiled=True)
    chosen_tiles = jnp.take(tiles[0], safe, axis=1)
    products = jnp.einsum(
        "ikpq,ikqf->ikpf", chosen_tiles, fetched, preferred_element_type=jnp.float32
    )
    live = valid[None, :] & (slot_ids[None, :] < tile_counts[0][:, None])
    products = jnp.where(live[:, :, None, None], products, jnp.zeros_like(products))
    target_rows = jnp.take(tile_rows[0], safe, axis=1).reshape(-1)
    accumulated = jnp.zeros((tiles_side, side, width), jnp.float32)
    accumulated = accumulated.at[target_rows].add(products.reshape(-1, side, width))
    flat = accumulated.reshape(block_rows, width)
    self_part = jnp.dot(out_grad, w_self.T, preferred_element_type=jnp.float32)
    contract = (((0,), (0,)), ((), ()))
    terms_self = lax.dot_general(features, out_grad, contract, preferred_element_type=jnp.float32)
    terms_neigh = lax.dot_general(
        aggregated, out_grad, contract, preferred_element_type=jnp.float32
    )
    scale = (out_grad.shape[0] * block_total * copies) ** (-0.5)
    spread_share = lax.psum_scatter(flat, "rep", scatter_dimension=0, tiled=True)
    self_sum, neigh_sum = lax.psum((terms_self, terms_neigh), ("blk", "rep"))
    return (spread_share + self_part, self_sum * scale, neigh_sum * scale)


def solution(mesh):
    blocks, copies = mesh.shape["blk"], mesh.shape["rep"]
    by_pairs = copies == 2 and blocks % (CORES * ROWS_Y) == 0
    placed = (
        P(("blk", "rep"), None),
        P(("blk", "rep"), None),
        P(("blk", "rep"), None),
        P(),
        P(),
        P("blk", None, None, None, None),
        P("blk", None, None),
        P("blk", None, None),
        P("blk", None),
    )
    return jax.shard_map(
        by_columns if by_pairs else on_device,
        mesh=mesh,
        in_specs=placed,
        out_specs=(P(("blk", "rep"), None), P(), P()),
        check_vma=False,
    )
```

```python
import functools

import jax
import jax.numpy as jnp
from jax import lax
from jax.experimental import pallas as pl
from jax.experimental.pallas import tpu as pltpu
from jax.sharding import PartitionSpec as P

MESH = pl.DeviceIdType.MESH
CORES, ROWS_Y = 2, 2


def gather_kernel(
    blocks,
    copies,
    scale,
    own_ref,
    other_ref,
    terms_ref,
    g_ref,
    sum_ref,
    parts,
    total,
    send_sem,
    recv_sem,
    x_sem,
    local_sem,
    part_send,
    part_recv,
    total_send,
    total_recv,
):
    b = lax.axis_index("blk")
    r = lax.axis_index("rep")
    line = blocks // (CORES * ROWS_Y)
    plane = CORES * ROWS_Y
    z, y, c = b // plane, (b // CORES) % ROWS_Y, b % CORES
    near_x = (b, 1 - r)
    near_core = (z * plane + y * CORES + (1 - c), r)
    near_y = (z * plane + (1 - y) * CORES + c, r)
    up, down = (b + plane, r), (b - plane, r)
    has_up, has_down = z < line - 1, z > 0

    barrier = pltpu.get_barrier_semaphore()
    devices = blocks * copies
    me = b * copies + r

    def peer_of(step):
        peer = (me + step) % devices
        return peer, (peer // copies, peer % copies)

    @pl.loop(1, devices)
    def _(step):
        pl.semaphore_signal(barrier, inc=1, device_id=peer_of(step)[1], device_id_type=MESH)

    pl.semaphore_wait(barrier, devices - 1)

    def part_copy(step):
        peer, device = peer_of(step)
        return pltpu.make_async_remote_copy(
            src_ref=terms_ref.at[peer],
            dst_ref=parts.at[me],
            send_sem=part_send.at[peer],
            recv_sem=part_recv.at[me],
            device_id=device,
            device_id_type=MESH,
        )

    def part_from(step):
        peer, device = peer_of(step)
        return pltpu.make_async_remote_copy(
            src_ref=terms_ref.at[peer],
            dst_ref=parts.at[peer],
            send_sem=part_send.at[peer],
            recv_sem=part_recv.at[peer],
            device_id=device,
            device_id_type=MESH,
        )

    def total_copy(step, slot):
        peer, device = peer_of(step)
        return pltpu.make_async_remote_copy(
            src_ref=total.at[me],
            dst_ref=total.at[slot],
            send_sem=total_send.at[peer],
            recv_sem=total_recv.at[slot],
            device_id=device,
            device_id_type=MESH,
        )

    def add_parts():
        parts[me] = terms_ref[me]

        @pl.loop(1, devices)
        def _(step):
            part_from(step).wait_recv()

        total[me] = jnp.sum(parts[...], axis=0) * scale

        @pl.loop(1, devices)
        def _(step):
            total_copy(step, me).start()

    def send(src, block, share, way, device):
        return pltpu.make_async_remote_copy(
            src_ref=src,
            dst_ref=g_ref.at[block, share],
            send_sem=send_sem.at[way, block, share],
            recv_sem=recv_sem.at[block, share],
            device_id=device,
            device_id_type=MESH,
        )

    def arrived(block, share):
        send(g_ref.at[block, share], block, share, 0, near_core).wait_recv()

    x_copy = pltpu.make_async_remote_copy(
        src_ref=other_ref,
        dst_ref=g_ref.at[b, r],
        send_sem=x_sem,
        recv_sem=recv_sem.at[b, r],
        device_id=near_x,
        device_id_type=MESH,
    )
    x_copy.start()
    keep = pltpu.make_async_copy(own_ref, g_ref.at[b, r], local_sem)
    keep.start()

    def spread_out(src, block, share, go_up, go_down):
        @pl.when(go_up)
        def _():
            send(src, block, share, 0, up).start()

        @pl.when(go_down)
        def _():
            send(src, block, share, 1, down).start()

        send(src, block, share, 2, near_y).start()
        send(src, block, share, 3, near_core).start()

    shares = (r, 1 - r)
    never = z < 0
    spread_out(own_ref, b, r, has_up, has_down)

    @pl.loop(1, devices)
    def _(step):
        part_copy(step).start()

    arrived(b, 1 - r)
    spread_out(g_ref.at[b, 1 - r], b, 1 - r, has_up, has_down)

    def from_y(distance, share):
        for sign in (-1, 1) if distance else (0,):
            other = z + sign * distance

            @pl.when((other >= 0) & (other < line))
            def _():
                block = other * plane + (1 - y) * CORES + c
                arrived(block, share)
                send(g_ref.at[block, share], block, share, 3, near_core).start()

    for distance in range(1, line):
        for share in shares:

            @pl.when(z - distance >= 0)
            def _():
                block = b - distance * plane
                arrived(block, share)
                spread_out(g_ref.at[block, share], block, share, has_up, never)

            @pl.when(z + distance < line)
            def _():
                block = b + distance * plane
                arrived(block, share)
                spread_out(g_ref.at[block, share], block, share, never, has_down)

        for share in shares:
            from_y(distance - 1, share)
        if distance == 1:
            add_parts()
    for share in shares:
        from_y(line - 1, share)

    @pl.loop(1, devices)
    def _(step):
        part_copy(step).wait_send()
        total_copy(step, me).wait_send()
        total_copy(step, peer_of(step)[0]).wait_recv()

    sum_ref[...] = total[...]
    keep.wait()
    x_copy.wait_send()
    for zz in range(line):
        for share in shares:
            for yy in (y, 1 - y):
                mine = zz * plane + yy * CORES + c
                arrived(zz * plane + yy * CORES + (1 - c), share)
                send(own_ref, mine, share, 3, near_core).wait_send()
            block = zz * plane + y * CORES + c
            send(own_ref, block, share, 2, near_y).wait_send()

            @pl.when((zz <= z) & has_up)
            def _():
                send(own_ref, block, share, 0, up).wait_send()

            @pl.when((zz >= z) & has_down)
            def _():
                send(own_ref, block, share, 1, down).wait_send()


def gather(own, other, terms, scale, blocks, copies):
    devices = blocks * copies
    rows, width = own.shape
    return pl.pallas_call(
        functools.partial(gather_kernel, blocks, copies, scale),
        out_shape=(
            jax.ShapeDtypeStruct((blocks, copies, rows, width), own.dtype),
            jax.ShapeDtypeStruct(terms.shape, terms.dtype),
        ),
        in_specs=[pl.BlockSpec(memory_space=pltpu.VMEM)] * 3,
        out_specs=(
            pl.BlockSpec(memory_space=pl.ANY),
            pl.BlockSpec(memory_space=pltpu.VMEM),
        ),
        scratch_shapes=[
            pltpu.VMEM(terms.shape, terms.dtype),
            pltpu.VMEM(terms.shape, terms.dtype),
            pltpu.SemaphoreType.DMA((4, blocks, copies)),
            pltpu.SemaphoreType.DMA((blocks, copies)),
            pltpu.SemaphoreType.DMA,
            pltpu.SemaphoreType.DMA,
            pltpu.SemaphoreType.DMA((devices,)),
            pltpu.SemaphoreType.DMA((devices,)),
            pltpu.SemaphoreType.DMA((devices,)),
            pltpu.SemaphoreType.DMA((devices,)),
        ],
        compiler_params=pltpu.CompilerParams(collective_id=0, has_side_effects=True),
        cost_estimate=pl.CostEstimate(
            flops=0, bytes_accessed=blocks * copies * rows * width * 20, transcendentals=0
        ),
    )(own, other, terms)


def spread_kernel(rows, cols, counts, tiles_ref, g_ref, o_ref):
    i = pl.program_id(0)
    slots, side = tiles_ref.shape[1], tiles_ref.shape[2]

    @pl.when(i == 0)
    def _():
        o_ref[...] = jnp.zeros_like(o_ref)

    products = []
    for k in range(slots):
        start = pl.multiple_of(cols[i * slots + k] * side, side)
        product = jnp.dot(
            tiles_ref[0, k], g_ref[0, pl.ds(start, side), :], preferred_element_type=jnp.float32
        )
        products.append(jnp.where(k < counts[i], product, jnp.zeros_like(product)))
    for k in range(slots):
        o_ref[rows[i * slots + k]] += products[k]


def spread_of(tiles, gathered, rows, cols, counts):
    blocks, slots, side, _ = tiles.shape
    depth, width = gathered.shape[1:]
    return pl.pallas_call(
        spread_kernel,
        out_shape=jax.ShapeDtypeStruct((depth // side, side, width), jnp.float32),
        grid_spec=pltpu.PrefetchScalarGridSpec(
            num_scalar_prefetch=3,
            grid=(blocks,),
            in_specs=[
                pl.BlockSpec((1, slots, side, side), lambda i, *_: (i, 0, 0, 0)),
                pl.BlockSpec((1, depth, width), lambda i, *_: (i, 0, 0)),
            ],
            out_specs=pl.BlockSpec((depth // side, side, width), lambda i, *_: (0, 0, 0)),
        ),
    )(rows.reshape(-1), cols.reshape(-1), counts.reshape(-1), tiles, gathered)


def by_columns(
    features, aggregated, out_grad, w_self, w_neigh, tiles, tile_rows, tile_cols, tile_counts
):
    blocks, copies = lax.axis_size("blk"), lax.axis_size("rep")
    r = lax.axis_index("rep")
    rows, width = out_grad.shape
    half = width // copies
    side = tiles.shape[-1]
    contract = (((0,), (0,)), ((), ()))
    devices = blocks * copies
    terms = jnp.concatenate(
        [
            lax.dot_general(a, out_grad, contract, preferred_element_type=jnp.float32)
            for a in (features, aggregated)
        ]
    )
    terms = terms.reshape(devices, -1, width)
    scale = (rows * devices) ** (-0.5)
    weights = w_neigh.reshape(copies, half, width)

    def message(which):
        chosen = lax.dynamic_index_in_dim(weights, which, 0, keepdims=False)
        return jnp.dot(out_grad, chosen.T, preferred_element_type=jnp.float32).astype(jnp.bfloat16)

    gathered, sums = gather(message(r), message(1 - r), terms, scale, blocks, copies)
    sums = sums.reshape(2, width, width)
    gathered = gathered.reshape(blocks, copies * rows, half)
    spread = spread_of(tiles[0], gathered, tile_rows[0], tile_cols[0], tile_counts[0])
    spread = spread.reshape(copies, rows, half)
    own = lax.dynamic_index_in_dim(spread, r, 0, keepdims=False)
    sent = lax.dynamic_index_in_dim(spread, 1 - r, 0, keepdims=False).astype(jnp.bfloat16)
    got = lax.ppermute(sent, "rep", [(0, 1), (1, 0)]).astype(jnp.float32)
    left, right = jnp.where(r == 0, own, got), jnp.where(r == 0, got, own)
    self_part = jnp.dot(out_grad, w_self.T, preferred_element_type=jnp.float32)
    feature_grad = self_part + jnp.concatenate([left, right], axis=1)
    return (feature_grad, sums[0], sums[1])


def on_device(
    features, aggregated, out_grad, w_self, w_neigh, tiles, tile_rows, tile_cols, tile_counts
):
    block_total = lax.axis_size("blk")
    copies = lax.axis_size("rep")
    replica = lax.axis_index("rep")
    width = out_grad.shape[1]
    side = tiles.shape[-1]
    slots_total = tiles.shape[2]
    share = jnp.dot(out_grad, w_neigh.T, preferred_element_type=jnp.float32).astype(jnp.bfloat16)
    whole = lax.all_gather(share, "rep", axis=0, tiled=True)
    block_rows = whole.shape[0]
    tiles_side = block_rows // side
    pieces_whole = whole.reshape(tiles_side, side, width)
    per_copy = (slots_total + copies - 1) // copies
    slot_ids = replica + copies * jnp.arange(per_copy, dtype=jnp.int32)
    valid = slot_ids < slots_total
    safe = jnp.minimum(slot_ids, slots_total - 1)
    wanted = jnp.take(tile_cols[0], safe, axis=1)
    found = pieces_whole[lax.all_to_all(wanted, "blk", split_axis=0, concat_axis=0, tiled=True)]
    fetched = lax.all_to_all(found, "blk", split_axis=0, concat_axis=0, tiled=True)
    chosen_tiles = jnp.take(tiles[0], safe, axis=1)
    products = jnp.einsum(
        "ikpq,ikqf->ikpf", chosen_tiles, fetched, preferred_element_type=jnp.float32
    )
    live = valid[None, :] & (slot_ids[None, :] < tile_counts[0][:, None])
    products = jnp.where(live[:, :, None, None], products, jnp.zeros_like(products))
    target_rows = jnp.take(tile_rows[0], safe, axis=1).reshape(-1)
    accumulated = jnp.zeros((tiles_side, side, width), jnp.float32)
    accumulated = accumulated.at[target_rows].add(products.reshape(-1, side, width))
    flat = accumulated.reshape(block_rows, width)
    self_part = jnp.dot(out_grad, w_self.T, preferred_element_type=jnp.float32)
    contract = (((0,), (0,)), ((), ()))
    terms_self = lax.dot_general(features, out_grad, contract, preferred_element_type=jnp.float32)
    terms_neigh = lax.dot_general(
        aggregated, out_grad, contract, preferred_element_type=jnp.float32
    )
    scale = (out_grad.shape[0] * block_total * copies) ** (-0.5)
    spread_share = lax.psum_scatter(flat, "rep", scatter_dimension=0, tiled=True)
    self_sum, neigh_sum = lax.psum((terms_self, terms_neigh), ("blk", "rep"))
    return (spread_share + self_part, self_sum * scale, neigh_sum * scale)


def solution(mesh):
    blocks, copies = mesh.shape["blk"], mesh.shape["rep"]
    by_pairs = copies == 2 and blocks % (CORES * ROWS_Y) == 0
    placed = (
        P(("blk", "rep"), None),
        P(("blk", "rep"), None),
        P(("blk", "rep"), None),
        P(),
        P(),
        P("blk", None, None, None, None),
        P("blk", None, None),
        P("blk", None, None),
        P("blk", None),
    )
    return jax.shard_map(
        by_columns if by_pairs else on_device,
        mesh=mesh,
        in_specs=placed,
        out_specs=(P(("blk", "rep"), None), P(), P()),
        check_vma=False,
    )
```
